32 devices in a mesh: ctx: 16 (over z, y, x), head: 2 (over core).
Axes of the slice: x: 2, y: 2, z: 4, core: 2. Of those that a mesh axis runs over, the one named last changes fastest.
Arguments:
- hidden_in: bfloat16 [8192, 8192], P('ctx', 'head'), may hold values from -6 to 6
- query: bfloat16 [8192, 8192], P('ctx', 'head'), may hold values from -6 to 6
- key: bfloat16 [8192, 1024], P('ctx', 'head'), may hold values from -6 to 6
- value: bfloat16 [8192, 1024], P('ctx', 'head'), may hold values from -6 to 6
- output_gradient: bfloat16 [8192, 8192], P('ctx', 'head'), may hold values from -6 to 6
- adapter_down: bfloat16 [48, 8192], P(None, 'head'), may hold values from -0.0625 to 0.0625
- up_query: bfloat16 [16, 8192], P(None, 'head'), may hold values from -0.0625 to 0.0625
- key_value_up_weight: bfloat16 [32, 1024], P(None, 'head'), may hold values from -0.1875 to 0.1875
Outputs:
- grad_query: bfloat16 [8192, 8192], P('ctx', 'head')
- key_gradient: bfloat16 [8192, 1024], P('ctx', 'head')
- value_gradient: bfloat16 [8192, 1024], P('ctx', 'head')
- grad_down: float32 [48, 8192], P(None, 'head')
- grad_up_query: float32 [16, 8192], P(None, 'head')
- grad_up_kv: float32 [32, 1024], P(None, 'head')
The draws below stay inside these ranges and needn't reach their ends.
All inputs are finite; a program needn't handle non-finite values.
Results may differ from the reference program's by a relative error of at most 0.014.
Values may be sent and summed in bfloat16 or wider, within the bound.
A program may use at most 128 MiB of HBM per device.

```python
import math
import jax
import jax.numpy as jnp
from jax import lax

D = 8192
QUERY_HEADS = 64
KEY_VALUE_HEADS = 8
HEAD_WIDTH = 128
ADAPTER_RANK = 16
TOKENS_PER_INDEX = 512
SEQUENCE_TOKENS = 8192


def levels(own_key, shape, split, low, largest):
    factor_of, own = 1.0, jax.random.fold_in(own_key, 6)
    for axis_at, blocks in split:
        steps = jnp.exp(jax.random.uniform(jax.random.fold_in(own, axis_at), (blocks,), jnp.float32, low / len(split), largest / len(split)))
        factor_of = factor_of * jnp.repeat(steps, shape[axis_at] // blocks).reshape([-1 if axis == axis_at else 1 for axis in range(len(shape))])
    return factor_of


def bell_draw(key, dims, deviation, limit, split=(), kind=jnp.bfloat16):
    values = jax.random.normal(key, dims, jnp.float32) * deviation
    if len(split) > 0:
        values = levels(key, dims, split, -0.22, 0.18) * values
    return jnp.clip(values, min=-limit, max=limit).astype(kind)


def setup_inputs(seed: int = 0) -> dict:
    splits = jax.random.split(jax.random.key(seed), 9)
    hidden_in = bell_draw(splits[0], (SEQUENCE_TOKENS, D), 1.0, 6.0, ((0, 16), (1, 2)))
    query = bell_draw(splits[1], (SEQUENCE_TOKENS, QUERY_HEADS * HEAD_WIDTH), 1.0, 6.0, ((0, 16), (1, 2)))
    key = bell_draw(splits[2], (SEQUENCE_TOKENS, KEY_VALUE_HEADS * HEAD_WIDTH), 1.0, 6.0, ((0, 16), (1, 2)))
    value = bell_draw(splits[3], (SEQUENCE_TOKENS, KEY_VALUE_HEADS * HEAD_WIDTH), 1.0, 6.0, ((0, 16), (1, 2)))
    output_gradient = bell_draw(splits[4], (SEQUENCE_TOKENS, QUERY_HEADS * HEAD_WIDTH), 1.0, 6.0, ((0, 16), (1, 2)))
    adapter_down = bell_draw(splits[5], (3 * ADAPTER_RANK, D), D ** -0.5, 0.0625, ((1, 2),))
    up_query = bell_draw(splits[6], (ADAPTER_RANK, QUERY_HEADS * HEAD_WIDTH), (QUERY_HEADS * HEAD_WIDTH) ** -0.5, 0.0625, ((1, 2),))
    key_value_up_weight = bell_draw(splits[7], (2 * ADAPTER_RANK, KEY_VALUE_HEADS * HEAD_WIDTH), (KEY_VALUE_HEADS * HEAD_WIDTH) ** -0.5, 0.1875, ((1, 2),))
    return {"hidden_in": hidden_in, "query": query, "key": key, "value": value, "output_gradient": output_gradient, "adapter_down": adapter_down, "up_query": up_query, "key_value_up_weight": key_value_up_weight}


def rounded(value):
    return lax.optimization_barrier(value.astype(jnp.bfloat16)).astype(jnp.float32)

def block_states(pieces):
    rows_of_queries, gradient_rows, rows_of_keys, rows_of_values = pieces
    state_kv = jnp.einsum('sjd,sje->jde', rows_of_keys.astype(jnp.float32), rows_of_values.astype(jnp.float32))
    state_qo = jnp.einsum('tjgd,tjge->jde', rows_of_queries.astype(jnp.float32), gradient_rows.astype(jnp.float32))
    return (state_kv, state_qo)

def reference(hidden_in, query, key, value, output_gradient, adapter_down, up_query, key_value_up_weight):
    query_group_width = QUERY_HEADS // KEY_VALUE_HEADS
    number_of_blocks = SEQUENCE_TOKENS // TOKENS_PER_INDEX
    att_scale = 1.0 / math.sqrt(HEAD_WIDTH * SEQUENCE_TOKENS)
    grad_scale = 1.0 / math.sqrt(SEQUENCE_TOKENS)
    rows_of_queries = query.reshape(number_of_blocks, TOKENS_PER_INDEX, KEY_VALUE_HEADS, query_group_width, HEAD_WIDTH)
    gradient_rows = output_gradient.reshape(number_of_blocks, TOKENS_PER_INDEX, KEY_VALUE_HEADS, query_group_width, HEAD_WIDTH)
    rows_of_keys = key.reshape(number_of_blocks, TOKENS_PER_INDEX, KEY_VALUE_HEADS, HEAD_WIDTH)
    rows_of_values = value.reshape(number_of_blocks, TOKENS_PER_INDEX, KEY_VALUE_HEADS, HEAD_WIDTH)
    state_kv, state_qo = lax.map(block_states, (rows_of_queries, gradient_rows, rows_of_keys, rows_of_values))
    initial_state = jnp.zeros((1, KEY_VALUE_HEADS, HEAD_WIDTH, HEAD_WIDTH), jnp.float32)
    prefix = jnp.concatenate([initial_state, jnp.cumsum(state_kv, axis=0)[:-1]], axis=0).astype(jnp.bfloat16)
    suffix = jnp.concatenate([jnp.cumsum(state_qo[::-1], axis=0)[::-1][1:], initial_state], axis=0).astype(jnp.bfloat16)
    causal = jnp.arange(TOKENS_PER_INDEX)[None, :] <= jnp.arange(TOKENS_PER_INDEX)[:, None]

    def one_block(pieces):
        q_rows, d_rows, k_rows, v_rows, pre_state, suf_state = pieces
        q_full = q_rows.astype(jnp.float32)
        d_full = d_rows.astype(jnp.float32)
        k_full = k_rows.astype(jnp.float32)
        v_full = v_rows.astype(jnp.float32)
        pre_full = pre_state.astype(jnp.float32)
        suf_full = suf_state.astype(jnp.float32)
        score_do = rounded(jnp.where(causal, jnp.einsum('tjgd,sjd->jgts', d_full, v_full), 0.0))
        score_qk = rounded(jnp.where(causal, jnp.einsum('tjgd,sjd->jgts', q_full, k_full), 0.0))
        grad_q = jnp.einsum('jgts,sjd->tjgd', score_do, k_full) + jnp.einsum('tjge,jde->tjgd', d_full, pre_full)
        key_gradient_part = jnp.einsum('jgts,tjgd->sjd', score_do, q_full) + jnp.einsum('sje,jde->sjd', v_full, suf_full)
        value_gradient_part = jnp.einsum('jgts,tjge->sje', score_qk, d_full) + jnp.einsum('sjd,jde->sje', k_full, suf_full)
        return ((att_scale * grad_q).astype(jnp.bfloat16), (att_scale * key_gradient_part).astype(jnp.bfloat16), (att_scale * value_gradient_part).astype(jnp.bfloat16))
    grad_q, key_gradient_part, value_gradient_part = lax.map(one_block, (rows_of_queries, gradient_rows, rows_of_keys, rows_of_values, prefix, suffix))
    grad_query = grad_q.reshape(SEQUENCE_TOKENS, QUERY_HEADS * HEAD_WIDTH)
    key_gradient = key_gradient_part.reshape(SEQUENCE_TOKENS, KEY_VALUE_HEADS * HEAD_WIDTH)
    value_gradient = value_gradient_part.reshape(SEQUENCE_TOKENS, KEY_VALUE_HEADS * HEAD_WIDTH)
    low = jnp.dot(hidden_in, adapter_down.T, preferred_element_type=jnp.float32).astype(jnp.bfloat16)
    back = jnp.concatenate([jnp.dot(grad_query, up_query.T, preferred_element_type=jnp.float32), jnp.dot(key_gradient, key_value_up_weight[:ADAPTER_RANK].T, preferred_element_type=jnp.float32), jnp.dot(value_gradient, key_value_up_weight[ADAPTER_RANK:].T, preferred_element_type=jnp.float32)], axis=1).astype(jnp.bfloat16)
    grad_down = grad_scale * jnp.dot(back.T, hidden_in, preferred_element_type=jnp.float32)
    grad_up_query = grad_scale * jnp.dot(low[:, :ADAPTER_RANK].T, grad_query, preferred_element_type=jnp.float32)
    grad_up_kv = grad_scale * jnp.concatenate([jnp.dot(low[:, ADAPTER_RANK:2 * ADAPTER_RANK].T, key_gradient, preferred_element_type=jnp.float32), jnp.dot(low[:, 2 * ADAPTER_RANK:].T, value_gradient, preferred_element_type=jnp.float32)], axis=0)
    return (grad_query, key_gradient, value_gradient, grad_down, grad_up_query, grad_up_kv)
```

```python
import functools
import math

import jax
import jax.numpy as jnp
from jax import lax
from jax.experimental import pallas as pl
from jax.experimental.pallas import tpu as pltpu
from jax.sharding import PartitionSpec as P

QUERY_HEADS = 64
KEY_VALUE_HEADS = 8
W = 128
RANK = 16
GROUP = QUERY_HEADS // KEY_VALUE_HEADS
BF = jnp.bfloat16
F32 = jnp.float32


def nn(a, b):
    return lax.dot_general(a, b, (((1,), (0,)), ((), ())), preferred_element_type=F32)


def nt(a, b):
    return lax.dot_general(a, b, (((1,), (1,)), ((), ())), preferred_element_type=F32)


def tn(a, b):
    return lax.dot_general(a, b, (((0,), (0,)), ((), ())), preferred_element_type=F32)


def dims_of(rows, cols, kv_cols, n):
    kvl = kv_cols // W
    state_rows = kvl * W
    chunk_rows = max(16, state_rows // n)
    chunk_cols = max(128, cols // n)
    return kvl, chunk_rows, state_rows // chunk_rows, chunk_cols, cols // chunk_cols


def kernel(
    n, nh, att_scale, grad_scale,
    hid_hbm, q_hbm, k_hbm, v_hbm, do_hbm, ad_hbm, uq_hbm, ukv_hbm,
    gq_hbm, dk_hbm, dv_hbm, down_out, upq_out, upkv_out,
    hid, q, k, v, do, ad, uq, ukv, gq, dk, dv,
    skv, sqo, st, recv1, res, pre,
    lowp, lowr, lowt, backp, backr, backt,
    rsbuf, rsrecv, ag, kvbuf, kvrecv, agkv,
    in_sem, out_sem, s1, r1, s2, r2, s3, r3, s4, r4, s5, r5, s6, r6, s7, r7, s8, r8,
):
    rows, cols = hid.shape
    kvl, R, own_st, cc, own_cc = dims_of(rows, cols, k.shape[1], n)
    sub = min(256, rows)
    nsub = rows // sub
    gw = GROUP * W
    me = lax.axis_index("ctx")
    mh = lax.axis_index("head")

    def gcols(j):
        return pl.ds(pl.multiple_of(j * gw, gw), gw)

    def jcols(j):
        return pl.ds(pl.multiple_of(j * W, W), W)

    def hcols(j, g):
        return pl.ds(pl.multiple_of(j * gw + g * W, W), W)

    def cchunk(o):
        return pl.ds(pl.multiple_of(o * cc, cc), cc)

    def rchunk(o):
        return pl.ds(pl.multiple_of(o * R, R), R)

    def cp(src, dst, i):
        return pltpu.make_async_copy(src, dst, in_sem.at[i])

    def cp_q(j):
        return cp(q_hbm.at[:, gcols(j)], q.at[:, gcols(j)], 6 + j)

    def cp_do(j):
        return cp(do_hbm.at[:, gcols(j)], do.at[:, gcols(j)], 6 + kvl + j)

    cp_k, cp_v = cp(k_hbm, k, 0), cp(v_hbm, v, 1)
    cp_hid, cp_ad = cp(hid_hbm, hid, 2), cp(ad_hbm, ad, 3)
    cp_uq, cp_ukv = cp(uq_hbm, uq, 4), cp(ukv_hbm, ukv, 5)

    cp_k.start()
    cp_v.start()
    for j in range(kvl):
        cp_q(j).start()
        cp_do(j).start()
    cp_ad.start()
    cp_hid.start()
    cp_uq.start()
    cp_ukv.start()

    barrier = pltpu.get_barrier_semaphore()

    @pl.loop(1, n)
    def _(i):
        pl.semaphore_signal(barrier, inc=1, device_id={"ctx": lax.rem(me + i, n)}, device_id_type=pl.DeviceIdType.MESH)

    for i in range(1, nh):
        pl.semaphore_signal(barrier, inc=1, device_id={"head": lax.rem(mh + i, nh)}, device_id_type=pl.DeviceIdType.MESH)

    def ctx_copy(src, dst, ssem, rsem, peer):
        return pltpu.make_async_remote_copy(
            src_ref=src, dst_ref=dst, send_sem=ssem, recv_sem=rsem,
            device_id={"ctx": peer}, device_id_type=pl.DeviceIdType.MESH,
        )

    def head_copy(src, dst, ssem, rsem, peer):
        return pltpu.make_async_remote_copy(
            src_ref=src, dst_ref=dst, send_sem=ssem, recv_sem=rsem,
            device_id={"head": peer}, device_id_type=pl.DeviceIdType.MESH,
        )

    def maybe(always, cond, fn):
        if always:
            fn()
        else:
            pl.when(cond)(fn)

    cp_k.wait()
    cp_v.wait()

    @pl.loop(0, kvl)
    def _(j):
        cp_q(j).wait()
        cp_do(j).wait()
        total_kv, total_qo = None, None
        jr = pl.ds(pl.multiple_of(j * W, W), W)
        for s in range(nsub):
            sr = pl.ds(s * sub, sub)
            a = tn(k[sr, jcols(j)], v[sr, jcols(j)])
            b = None
            for g in range(GROUP):
                t = tn(q[sr, hcols(j, g)], do[sr, hcols(j, g)])
                b = t if b is None else b + t
            skv[s, jr, :] = a
            sqo[s, jr, :] = b
            total_kv = a if total_kv is None else total_kv + a
            total_qo = b if total_qo is None else total_qo + b
        st[0, jr, :] = total_kv.astype(BF)
        st[1, jr, :] = total_qo.astype(BF)

    pl.semaphore_wait(barrier, n - 1 + nh - 1)

    def scan_send(i):
        peer = lax.rem(me + i, n)
        return peer, ctx_copy(st.at[:, rchunk(peer), :], recv1.at[me], s1.at[i], r1.at[me], peer)

    @pl.loop(1, n)
    def _(i):
        peer, c = scan_send(i)
        maybe(own_st == n, peer < own_st, lambda: c.start())

    cp_ad.wait()
    cp_hid.wait()
    lowp[...] = nt(ad[...], hid[...]).astype(BF)
    for i in range(1, nh):
        peer = lax.rem(mh + i, nh)
        head_copy(lowp, lowr.at[mh], s3.at[i], r3.at[mh], peer).start()

    below = lax.broadcasted_iota(jnp.int32, (sub, sub), 0)
    right = lax.broadcasted_iota(jnp.int32, (sub, sub), 1)

    def intra(j, s):
        sr = pl.ds(s * sub, sub)
        kk, vv = k[sr, jcols(j)], v[sr, jcols(j)]
        sum_k, sum_v = None, None
        for g in range(GROUP):
            qq, dd = q[sr, hcols(j, g)], do[sr, hcols(j, g)]
            sd = jnp.where(below <= right, nt(vv, dd), 0.0).astype(BF)
            sq = jnp.where(below <= right, nt(kk, qq), 0.0).astype(BF)
            a, b = nn(sd, qq), nn(sq, dd)
            sum_k = a if sum_k is None else sum_k + a
            sum_v = b if sum_v is None else sum_v + b
        return sum_k, sum_v

    acc_k, acc_v = dk, dv
    first = (kvl + 1) // 2

    def intra_j(j):
        for s in range(nsub):
            sr = pl.ds(s * sub, sub)
            a, b = intra(j, s)
            acc_k[sr, jcols(j)] = a
            acc_v[sr, jcols(j)] = b

    pl.loop(0, first)(intra_j)

    def scan_owner():
        recv1[me] = st[:, rchunk(me), :]

        @pl.loop(1, n)
        def _(i):
            p = lax.rem(me + n - i, n)
            ctx_copy(st.at[:, pl.ds(0, R), :], recv1.at[p], s1.at[i], r1.at[p], p).wait_recv()

        def forward(b, run):
            res[b, 0] = run.astype(BF)
            return run + recv1[b, 0].astype(F32)

        def backward(b, run):
            at = n - 1 - b
            res[at, 1] = run.astype(BF)
            return run + recv1[at, 1].astype(F32)

        zero = jnp.zeros((R, W), F32)
        lax.fori_loop(0, n, forward, zero)
        lax.fori_loop(0, n, backward, zero)
        pre[:, rchunk(me), :] = res[me]

        @pl.loop(1, n)
        def _(i):
            p = lax.rem(me + i, n)
            ctx_copy(res.at[p], pre.at[:, rchunk(me), :], s2.at[i], r2.at[me], p).start()

    maybe(own_st == n, me < own_st, scan_owner)

    pl.loop(first, kvl)(intra_j)

    @pl.loop(1, n)
    def _(i):
        p = lax.rem(me + n - i, n)
        c = ctx_copy(res.at[0], pre.at[:, rchunk(p), :], s2.at[i], r2.at[p], p)
        maybe(own_st == n, p < own_st, lambda: c.wait_recv())

    lowr[mh] = lowp[...]
    for i in range(1, nh):
        peer = lax.rem(mh + nh - i, nh)
        head_copy(lowp, lowr.at[peer], s3.at[i], r3.at[peer], peer).wait_recv()
    total = lowr[0].astype(F32)
    for i in range(1, nh):
        total = total + lowr[i].astype(F32)
    lowt[...] = total.astype(BF)

    cp_uq.wait()
    cp_ukv.wait()

    def cp_gq(j):
        return pltpu.make_async_copy(gq.at[:, gcols(j)], gq_hbm.at[:, gcols(j)], out_sem.at[2 + j])

    backp[...] = jnp.zeros_like(backp)

    @pl.loop(0, kvl)
    def _(j):
        jr = pl.ds(pl.multiple_of(j * W, W), W)
        pfx = pre[0, jr, :].astype(F32)
        for s in range(nsub):
            sr = pl.ds(s * sub, sub)
            kk, vv = k[sr, jcols(j)], v[sr, jcols(j)]
            here = pfx.astype(BF)
            for g in range(GROUP):
                dd = do[sr, hcols(j, g)]
                sd = jnp.where(right <= below, nt(dd, vv), 0.0).astype(BF)
                out = nn(sd, kk) + nt(dd, here)
                gq[sr, hcols(j, g)] = (att_scale * out).astype(BF)
            if s + 1 < nsub:
                pfx = pfx + skv[s, jr, :]
        sfx = pre[1, jr, :].astype(F32)
        for s in reversed(range(nsub)):
            sr = pl.ds(s * sub, sub)
            kk, vv = k[sr, jcols(j)], v[sr, jcols(j)]
            here = sfx.astype(BF)
            a = acc_k[sr, jcols(j)] + nt(vv, here)
            b = acc_v[sr, jcols(j)] + nn(kk, here)
            k_out = (att_scale * a).astype(BF)
            v_out = (att_scale * b).astype(BF)
            k[sr, jcols(j)] = k_out
            v[sr, jcols(j)] = v_out
            if s > 0:
                sfx = sfx + sqo[s, jr, :]
        cp_gq(j).start()
        backp[pl.ds(0, RANK), :] += nt(uq[:, gcols(j)], gq[:, gcols(j)])
        backp[pl.ds(RANK, RANK), :] += nt(ukv[pl.ds(0, RANK), jcols(j)], k[:, jcols(j)])
        backp[pl.ds(2 * RANK, RANK), :] += nt(ukv[pl.ds(RANK, RANK), jcols(j)], v[:, jcols(j)])
        kvbuf[j, pl.ds(0, RANK), :] = nn(lowt[pl.ds(RANK, RANK), :], k[:, jcols(j)]).astype(BF)
        kvbuf[j, pl.ds(RANK, RANK), :] = nn(lowt[pl.ds(2 * RANK, RANK), :], v[:, jcols(j)]).astype(BF)

    cp_dk = pltpu.make_async_copy(k, dk_hbm, out_sem.at[0])
    cp_dv = pltpu.make_async_copy(v, dv_hbm, out_sem.at[1])
    cp_dk.start()
    cp_dv.start()

    backr[mh] = backp[...].astype(BF)
    for i in range(1, nh):
        peer = lax.rem(mh + i, nh)
        head_copy(backr.at[mh], backr.at[mh], s4.at[i], r4.at[mh], peer).start()

    def kv_send(j):
        return ctx_copy(kvbuf.at[j], kvrecv.at[me], s7.at[j], r7.at[me], j)

    for j in range(kvl):
        pl.when(me != j)(lambda: kv_send(j).start())

    @pl.loop(0, own_cc)
    def _(o):
        rsbuf[o, pl.ds(3 * RANK, RANK), :] = nn(lowt[pl.ds(0, RANK), :], gq[:, cchunk(o)]).astype(BF)

    for i in range(1, nh):
        peer = lax.rem(mh + nh - i, nh)
        head_copy(backr.at[mh], backr.at[peer], s4.at[i], r4.at[peer], peer).wait_recv()
    total = backr[0].astype(F32)
    for i in range(1, nh):
        total = total + backr[i].astype(F32)
    backt[...] = total.astype(BF)

    def rs_send(i):
        o = lax.rem(me + i, n)
        return o, ctx_copy(rsbuf.at[o], rsrecv.at[me], s5.at[i], r5.at[me], o)

    def down(o):
        rsbuf[o, pl.ds(0, 3 * RANK), :] = nn(backt[...], hid[:, cchunk(o)]).astype(BF)

    @pl.loop(1, n)
    def _(i):
        o, c = rs_send(i)

        def go():
            down(o)
            c.start()

        maybe(own_cc == n, o < own_cc, go)

    def rs_own():
        down(me)
        rsrecv[me] = rsbuf[me]

        def add(i, acc):
            p = lax.rem(me + n - i, n)
            ctx_copy(rsbuf.at[0], rsrecv.at[p], s5.at[i], r5.at[p], p).wait_recv()
            return acc + rsrecv[p].astype(F32)

        acc = lax.fori_loop(1, n, add, rsrecv[me].astype(F32))
        ag[me] = (grad_scale * acc).astype(BF)

        @pl.loop(1, n)
        def _(i):
            p = lax.rem(me + i, n)
            ctx_copy(ag.at[me], ag.at[me], s6.at[i], r6.at[me], p).start()

    maybe(own_cc == n, me < own_cc, rs_own)

    @pl.when(me < kvl)
    def _():
        kvrecv[me] = kvbuf[me]

        def add(i, acc):
            p = lax.rem(me + n - i, n)
            ctx_copy(kvbuf.at[0], kvrecv.at[p], s7.at[0], r7.at[p], p).wait_recv()
            return acc + kvrecv[p].astype(F32)

        acc = lax.fori_loop(1, n, add, kvrecv[me].astype(F32))
        agkv[me] = (grad_scale * acc).astype(BF)

        @pl.loop(1, n)
        def _(i):
            p = lax.rem(me + i, n)
            ctx_copy(agkv.at[me], agkv.at[me], s8.at[i], r8.at[me], p).start()

    def put(o):
        down_out[:, cchunk(o)] = ag[o, pl.ds(0, 3 * RANK), :].astype(F32)
        upq_out[:, cchunk(o)] = ag[o, pl.ds(3 * RANK, RANK), :].astype(F32)

    maybe(own_cc == n, me < own_cc, lambda: put(me))

    @pl.loop(1, n)
    def _(i):
        p = lax.rem(me + n - i, n)
        c = ctx_copy(ag.at[p], ag.at[p], s6.at[i], r6.at[p], p)

        def go():
            c.wait_recv()
            put(p)

        maybe(own_cc == n, p < own_cc, go)

    for j in range(kvl):
        pl.when(me != j)(
            lambda: ctx_copy(agkv.at[j], agkv.at[j], s8.at[0], r8.at[j], j).wait_recv()
        )
        upkv_out[:, pl.ds(j * W, W)] = agkv[j].astype(F32)

    @pl.loop(1, n)
    def _(i):
        peer, c = scan_send(i)
        maybe(own_st == n, peer < own_st, lambda: c.wait_send())
        o, c2 = rs_send(i)
        maybe(own_cc == n, o < own_cc, lambda: c2.wait_send())
        c3 = ctx_copy(res.at[peer], pre.at[:, rchunk(0), :], s2.at[i], r2.at[me], peer)
        maybe(own_st == n, me < own_st, lambda: c3.wait_send())
        c4 = ctx_copy(ag.at[0], ag.at[0], s6.at[i], r6.at[me], peer)
        maybe(own_cc == n, me < own_cc, lambda: c4.wait_send())

        @pl.when(me < kvl)
        def _():
            ctx_copy(agkv.at[0], agkv.at[0], s8.at[i], r8.at[me], peer).wait_send()

    for j in range(kvl):
        pl.when(me != j)(lambda: kv_send(j).wait_send())
    for i in range(1, nh):
        peer = lax.rem(mh + i, nh)
        head_copy(lowp, lowr.at[mh], s3.at[i], r3.at[mh], peer).wait_send()
        head_copy(backr.at[mh], backr.at[mh], s4.at[i], r4.at[mh], peer).wait_send()
    cp_dk.wait()
    cp_dv.wait()
    for j in range(kvl):
        cp_gq(j).wait()


def on_device(n, nh, hid, q, k, v, do, ad, uq, ukv):
    rows, cols = hid.shape
    kvl, R, own_st, cc, own_cc = dims_of(rows, cols, k.shape[1], n)
    nsub = rows // min(256, rows)
    total_tokens = rows * n
    any_spec = pl.BlockSpec(memory_space=pl.ANY)
    vmem_spec = pl.BlockSpec(memory_space=pltpu.VMEM)
    V = pltpu.VMEM
    dma = pltpu.SemaphoreType.DMA
    kw = k.shape[1]
    r3 = 3 * RANK
    return pl.pallas_call(
        functools.partial(
            kernel, n, nh, 1.0 / math.sqrt(W * total_tokens), 1.0 / math.sqrt(total_tokens)
        ),
        out_shape=(
            jax.ShapeDtypeStruct((rows, cols), BF),
            jax.ShapeDtypeStruct((rows, kw), BF),
            jax.ShapeDtypeStruct((rows, kw), BF),
            jax.ShapeDtypeStruct((r3, cols), F32),
            jax.ShapeDtypeStruct((RANK, cols), F32),
            jax.ShapeDtypeStruct((2 * RANK, kw), F32),
        ),
        in_specs=[any_spec] * 8,
        out_specs=(any_spec, any_spec, any_spec, vmem_spec, vmem_spec, vmem_spec),
        scratch_shapes=[
            V((rows, cols), BF), V((rows, cols), BF), V((rows, kw), BF), V((rows, kw), BF),
            V((rows, cols), BF), V(ad.shape, BF), V(uq.shape, BF), V(ukv.shape, BF),
            V((rows, cols), BF), V((rows, kw), F32), V((rows, kw), F32),
            V((nsub, kvl * W, W), F32), V((nsub, kvl * W, W), F32),
            V((2, kvl * W, W), BF), V((n, 2, R, W), BF), V((n, 2, R, W), BF), V((2, kvl * W, W), BF),
            V((r3, rows), BF), V((nh, r3, rows), BF), V((r3, rows), BF),
            V((r3, rows), F32), V((nh, r3, rows), BF), V((r3, rows), BF),
            V((own_cc, 4 * RANK, cc), BF), V((n, 4 * RANK, cc), BF), V((own_cc, 4 * RANK, cc), BF),
            V((kvl, 2 * RANK, W), BF), V((n, 2 * RANK, W), BF), V((kvl, 2 * RANK, W), BF),
            dma((6 + 2 * kvl,)), dma((2 + kvl,)),
            dma((n,)), dma((n,)), dma((n,)), dma((n,)),
            dma((nh,)), dma((nh,)), dma((nh,)), dma((nh,)),
            dma((n,)), dma((n,)), dma((n,)), dma((n,)),
            dma((max(n, kvl),)), dma((n,)), dma((n,)), dma((max(n, kvl),)),
        ],
        compiler_params=pltpu.CompilerParams(
            collective_id=0, has_side_effects=True, vmem_limit_bytes=60 * 1024 * 1024
        ),
        name="linear_attention_backward",
    )(hid, q, k, v, do, ad, uq, ukv)


def solution(mesh):
    tok, feat = P("ctx", "head"), P(None, "head")
    return jax.shard_map(
        functools.partial(on_device, mesh.shape["ctx"], mesh.shape["head"]),
        mesh=mesh,
        in_specs=(tok, tok, tok, tok, tok, feat, feat, feat),
        out_specs=(tok, tok, tok, feat, feat, feat),
        check_vma=False,
    )
```

```python
import functools
import math

import jax
import jax.numpy as jnp
from jax import lax
from jax.experimental import pallas as pl
from jax.experimental.pallas import tpu as pltpu
from jax.sharding import PartitionSpec as P

QUERY_HEADS = 64
KEY_VALUE_HEADS = 8
W = 128
RANK = 16
GROUP = QUERY_HEADS // KEY_VALUE_HEADS
BF = jnp.bfloat16
F32 = jnp.float32


def nn(a, b):
    return lax.dot_general(a, b, (((1,), (0,)), ((), ())), preferred_element_type=F32)


def nt(a, b):
    return lax.dot_general(a, b, (((1,), (1,)), ((), ())), preferred_element_type=F32)


def tn(a, b):
    return lax.dot_general(a, b, (((0,), (0,)), ((), ())), preferred_element_type=F32)


def dims_of(rows, cols, kv_cols, n):
    kvl = kv_cols // W
    state_rows = kvl * W
    chunk_rows = max(16, state_rows // n)
    chunk_cols = max(128, cols // n)
    return kvl, chunk_rows, state_rows // chunk_rows, chunk_cols, cols // chunk_cols


def kernel(
    n, nh, att_scale, grad_scale,
    hid_hbm, q_hbm, k_hbm, v_hbm, do_hbm, ad_hbm, uq_hbm, ukv_hbm,
    gq_hbm, dk_hbm, dv_hbm, down_out, upq_out, upkv_out,
    hid, q, k, v, do, ad, uq, ukv, gq, dk, dv,
    skv, sqo, st, recv1, res, pre,
    lowp, lowr, lowt, backp, backr, backt,
    rsbuf, rsrecv, ag, uqbuf, uqrecv, aguq, kvbuf, kvrecv, agkv,
    in_sem, out_sem, s1, r1, s2, r2, s3, r3, s4, r4, s5, r5, s6, r6, s7, r7, s8, r8, s9, r9, sa, ra,
):
    rows, cols = hid.shape
    kvl, R, own_st, cc, own_cc = dims_of(rows, cols, k.shape[1], n)
    sub = min(256, rows)
    nsub = rows // sub
    gw = GROUP * W
    me = lax.axis_index("ctx")
    mh = lax.axis_index("head")

    def gcols(j):
        return pl.ds(pl.multiple_of(j * gw, gw), gw)

    def jcols(j):
        return pl.ds(pl.multiple_of(j * W, W), W)

    def hcols(j, g):
        return pl.ds(pl.multiple_of(j * gw + g * W, W), W)

    def cchunk(o):
        return pl.ds(pl.multiple_of(o * cc, cc), cc)

    def rchunk(o):
        return pl.ds(pl.multiple_of(o * R, R), R)

    def cp(src, dst, i):
        return pltpu.make_async_copy(src, dst, in_sem.at[i])

    def cp_q(j):
        return cp(q_hbm.at[:, gcols(j)], q.at[:, gcols(j)], 6 + j)

    def cp_do(j):
        return cp(do_hbm.at[:, gcols(j)], do.at[:, gcols(j)], 6 + kvl + j)

    cp_k, cp_v = cp(k_hbm, k, 0), cp(v_hbm, v, 1)
    cp_hid, cp_ad = cp(hid_hbm, hid, 2), cp(ad_hbm, ad, 3)
    cp_uq, cp_ukv = cp(uq_hbm, uq, 4), cp(ukv_hbm, ukv, 5)

    cp_k.start()
    cp_v.start()
    for j in range(kvl):
        cp_q(j).start()
        cp_do(j).start()
    cp_ad.start()
    cp_hid.start()
    cp_uq.start()
    cp_ukv.start()

    barrier = pltpu.get_barrier_semaphore()

    @pl.loop(1, n)
    def _(i):
        pl.semaphore_signal(barrier, inc=1, device_id={"ctx": lax.rem(me + i, n)}, device_id_type=pl.DeviceIdType.MESH)

    for i in range(1, nh):
        pl.semaphore_signal(barrier, inc=1, device_id={"head": lax.rem(mh + i, nh)}, device_id_type=pl.DeviceIdType.MESH)

    def ctx_copy(src, dst, ssem, rsem, peer):
        return pltpu.make_async_remote_copy(
            src_ref=src, dst_ref=dst, send_sem=ssem, recv_sem=rsem,
            device_id={"ctx": peer}, device_id_type=pl.DeviceIdType.MESH,
        )

    def head_copy(src, dst, ssem, rsem, peer):
        return pltpu.make_async_remote_copy(
            src_ref=src, dst_ref=dst, send_sem=ssem, recv_sem=rsem,
            device_id={"head": peer}, device_id_type=pl.DeviceIdType.MESH,
        )

    def far(t):
        return n // 2 + lax.div(t, 2) * (1 - 2 * lax.rem(t, 2))

    def maybe(always, cond, fn):
        if always:
            fn()
        else:
            pl.when(cond)(fn)

    cp_k.wait()
    cp_v.wait()

    per_head = own_st // kvl

    def scan_send(o):
        return ctx_copy(st.at[:, rchunk(o), :], recv1.at[me], s1.at[o], r1.at[me], o)

    @pl.loop(0, kvl)
    def _(j):
        cp_q(j).wait()
        cp_do(j).wait()
        total_kv, total_qo = None, None
        jr = pl.ds(pl.multiple_of(j * W, W), W)
        for s in range(nsub):
            sr = pl.ds(s * sub, sub)
            a = tn(k[sr, jcols(j)], v[sr, jcols(j)])
            b = None
            for g in range(GROUP):
                t = tn(q[sr, hcols(j, g)], do[sr, hcols(j, g)])
                b = t if b is None else b + t
            skv[s, jr, :] = a
            sqo[s, jr, :] = b
            total_kv = a if total_kv is None else total_kv + a
            total_qo = b if total_qo is None else total_qo + b
        st[0, jr, :] = total_kv.astype(BF)
        st[1, jr, :] = total_qo.astype(BF)

        @pl.when(j == 0)
        def _():
            pl.semaphore_wait(barrier, n - 1 + nh - 1)

        for t in range(per_head):
            o = j * per_head + lax.rem(me + t, per_head)
            pl.when(o != me)(lambda: scan_send(o).start())

    cp_ad.wait()
    cp_hid.wait()
    lowp[...] = nt(ad[...], hid[...]).astype(BF)
    for i in range(1, nh):
        peer = lax.rem(mh + i, nh)
        head_copy(lowp, lowr.at[mh], s3.at[i], r3.at[mh], peer).start()

    below = lax.broadcasted_iota(jnp.int32, (sub, sub), 0)
    right = lax.broadcasted_iota(jnp.int32, (sub, sub), 1)

    def intra(j, s):
        sr = pl.ds(s * sub, sub)
        kk, vv = k[sr, jcols(j)], v[sr, jcols(j)]
        sum_k, sum_v = None, None
        for g in range(GROUP):
            qq, dd = q[sr, hcols(j, g)], do[sr, hcols(j, g)]
            sd = jnp.where(below <= right, nt(vv, dd), 0.0).astype(BF)
            sq = jnp.where(below <= right, nt(kk, qq), 0.0).astype(BF)
            a, b = nn(sd, qq), nn(sq, dd)
            sum_k = a if sum_k is None else sum_k + a
            sum_v = b if sum_v is None else sum_v + b
        return sum_k, sum_v

    acc_k, acc_v = dk, dv
    first = (kvl + 1) // 2

    def intra_j(j):
        for s in range(nsub):
            sr = pl.ds(s * sub, sub)
            a, b = intra(j, s)
            acc_k[sr, jcols(j)] = a
            acc_v[sr, jcols(j)] = b

    pl.loop(0, first)(intra_j)

    def scan_owner():
        recv1[me] = st[:, rchunk(me), :]

        @pl.loop(1, n)
        def _(i):
            p = lax.rem(me + n - i, n)
            ctx_copy(st.at[:, pl.ds(0, R), :], recv1.at[p], s1.at[i], r1.at[p], p).wait_recv()

        def forward(b, run):
            res[b, 0] = run.astype(BF)
            return run + recv1[b, 0].astype(F32)

        def backward(b, run):
            at = n - 1 - b
            res[at, 1] = run.astype(BF)
            return run + recv1[at, 1].astype(F32)

        zero = jnp.zeros((R, W), F32)
        lax.fori_loop(0, n, forward, zero)
        lax.fori_loop(0, n, backward, zero)
        pre[:, rchunk(me), :] = res[me]

        @pl.loop(1, n)
        def _(t):
            i = far(t)
            p = lax.rem(me + i, n)
            ctx_copy(res.at[p], pre.at[:, rchunk(me), :], s2.at[i], r2.at[me], p).start()

    maybe(own_st == n, me < own_st, scan_owner)

    pl.loop(first, kvl)(intra_j)

    @pl.loop(1, n)
    def _(i):
        p = lax.rem(me + n - i, n)
        c = ctx_copy(res.at[0], pre.at[:, rchunk(p), :], s2.at[i], r2.at[p], p)
        maybe(own_st == n, p < own_st, lambda: c.wait_recv())

    lowr[mh] = lowp[...]
    for i in range(1, nh):
        peer = lax.rem(mh + nh - i, nh)
        head_copy(lowp, lowr.at[peer], s3.at[i], r3.at[peer], peer).wait_recv()
    total = lowr[0].astype(F32)
    for i in range(1, nh):
        total = total + lowr[i].astype(F32)
    lowt[...] = total.astype(BF)

    cp_uq.wait()
    cp_ukv.wait()

    def cp_gq(j):
        return pltpu.make_async_copy(gq.at[:, gcols(j)], gq_hbm.at[:, gcols(j)], out_sem.at[2 + j])

    backp[...] = jnp.zeros_like(backp)
    cuts = own_cc // kvl

    def kv_send(j):
        return ctx_copy(kvbuf.at[j], kvrecv.at[me], s7.at[j], r7.at[me], j)

    def uq_send(o):
        return ctx_copy(uqbuf.at[o], uqrecv.at[me], s9.at[o], r9.at[me], o)

    @pl.loop(0, kvl)
    def _(j):
        jr = pl.ds(pl.multiple_of(j * W, W), W)
        pfx = pre[0, jr, :].astype(F32)
        for s in range(nsub):
            sr = pl.ds(s * sub, sub)
            kk, vv = k[sr, jcols(j)], v[sr, jcols(j)]
            here = pfx.astype(BF)
            for g in range(GROUP):
                dd = do[sr, hcols(j, g)]
                sd = jnp.where(right <= below, nt(dd, vv), 0.0).astype(BF)
                out = nn(sd, kk) + nt(dd, here)
                gq[sr, hcols(j, g)] = (att_scale * out).astype(BF)
            if s + 1 < nsub:
                pfx = pfx + skv[s, jr, :]
        sfx = pre[1, jr, :].astype(F32)
        for s in reversed(range(nsub)):
            sr = pl.ds(s * sub, sub)
            kk, vv = k[sr, jcols(j)], v[sr, jcols(j)]
            here = sfx.astype(BF)
            a = acc_k[sr, jcols(j)] + nt(vv, here)
            b = acc_v[sr, jcols(j)] + nn(kk, here)
            k_out = (att_scale * a).astype(BF)
            v_out = (att_scale * b).astype(BF)
            k[sr, jcols(j)] = k_out
            v[sr, jcols(j)] = v_out
            if s > 0:
                sfx = sfx + sqo[s, jr, :]
        cp_gq(j).start()
        backp[pl.ds(0, RANK), :] += nt(uq[:, gcols(j)], gq[:, gcols(j)])
        backp[pl.ds(RANK, RANK), :] += nt(ukv[pl.ds(0, RANK), jcols(j)], k[:, jcols(j)])
        backp[pl.ds(2 * RANK, RANK), :] += nt(ukv[pl.ds(RANK, RANK), jcols(j)], v[:, jcols(j)])
        kvbuf[j, pl.ds(0, RANK), :] = nn(lowt[pl.ds(RANK, RANK), :], k[:, jcols(j)]).astype(BF)
        kvbuf[j, pl.ds(RANK, RANK), :] = nn(lowt[pl.ds(2 * RANK, RANK), :], v[:, jcols(j)]).astype(BF)
        pl.when(me != j)(lambda: kv_send(j).start())
        part = nn(lowt[pl.ds(0, RANK), :], gq[:, gcols(j)]).astype(BF)
        for t in range(cuts):
            uqbuf[j * cuts + t] = part[:, t * cc : (t + 1) * cc]
        for t in range(cuts):
            o = j * cuts + t
            pl.when(o != me)(lambda: uq_send(o).start())

    cp_dk = pltpu.make_async_copy(k, dk_hbm, out_sem.at[0])
    cp_dv = pltpu.make_async_copy(v, dv_hbm, out_sem.at[1])
    cp_dk.start()
    cp_dv.start()

    backr[mh] = backp[...].astype(BF)
    for i in range(1, nh):
        peer = lax.rem(mh + i, nh)
        head_copy(backr.at[mh], backr.at[mh], s4.at[i], r4.at[mh], peer).start()

    for i in range(1, nh):
        peer = lax.rem(mh + nh - i, nh)
        head_copy(backr.at[mh], backr.at[peer], s4.at[i], r4.at[peer], peer).wait_recv()
    total = backr[0].astype(F32)
    for i in range(1, nh):
        total = total + backr[i].astype(F32)
    backt[...] = total.astype(BF)

    def rs_send(i):
        o = lax.rem(me + i, n)
        return o, ctx_copy(rsbuf.at[o], rsrecv.at[me], s5.at[i], r5.at[me], o)

    def down(o):
        rsbuf[o] = nn(backt[...], hid[:, cchunk(o)]).astype(BF)

    @pl.loop(1, n)
    def _(t):
        o, c = rs_send(far(t))

        def go():
            down(o)
            c.start()

        maybe(own_cc == n, o < own_cc, go)

    def own_sum(mine, recv, gathered, s_in, r_in, s_out, r_out):
        recv[me] = mine[me]

        def add(t, acc):
            p = lax.rem(me + n - t, n)
            ctx_copy(mine.at[0], recv.at[p], s_in.at[0], r_in.at[p], p).wait_recv()
            return acc + recv[p].astype(F32)

        acc = lax.fori_loop(1, n, add, recv[me].astype(F32))
        gathered[me] = (grad_scale * acc).astype(BF)

        @pl.loop(1, n)
        def _(t):
            i = far(t)
            p = lax.rem(me + i, n)
            ctx_copy(gathered.at[me], gathered.at[me], s_out.at[i], r_out.at[me], p).start()

    maybe(own_cc == n, me < own_cc, lambda: down(me))
    maybe(own_cc == n, me < own_cc, lambda: own_sum(uqbuf, uqrecv, aguq, s9, r9, sa, ra))
    pl.when(me < kvl)(lambda: own_sum(kvbuf, kvrecv, agkv, s7, r7, s8, r8))
    maybe(own_cc == n, me < own_cc, lambda: own_sum(rsbuf, rsrecv, ag, s5, r5, s6, r6))

    def put_uq(o):
        upq_out[:, cchunk(o)] = aguq[o]

    def put(o):
        down_out[:, cchunk(o)] = ag[o]

    for j in range(kvl):
        pl.when(me != j)(
            lambda: ctx_copy(agkv.at[j], agkv.at[j], s8.at[0], r8.at[j], j).wait_recv()
        )
        upkv_out[:, pl.ds(j * W, W)] = agkv[j]

    maybe(own_cc == n, me < own_cc, lambda: put_uq(me))
    maybe(own_cc == n, me < own_cc, lambda: put(me))

    def collect(gathered, s_out, r_out, fn):
        @pl.loop(1, n)
        def _(i):
            p = lax.rem(me + n - i, n)

            def go():
                ctx_copy(gathered.at[p], gathered.at[p], s_out.at[i], r_out.at[p], p).wait_recv()
                fn(p)

            maybe(own_cc == n, p < own_cc, go)

    collect(aguq, sa, ra, put_uq)
    collect(ag, s6, r6, put)

    @pl.loop(1, n)
    def _(i):
        peer = lax.rem(me + i, n)
        maybe(own_st == n, peer < own_st, lambda: scan_send(peer).wait_send())
        maybe(own_cc == n, peer < own_cc, lambda: uq_send(peer).wait_send())
        o, c2 = rs_send(i)
        maybe(own_cc == n, o < own_cc, lambda: c2.wait_send())
        c3 = ctx_copy(res.at[peer], pre.at[:, rchunk(0), :], s2.at[i], r2.at[me], peer)
        maybe(own_st == n, me < own_st, lambda: c3.wait_send())
        c4 = ctx_copy(ag.at[0], ag.at[0], s6.at[i], r6.at[0], peer)
        maybe(own_cc == n, me < own_cc, lambda: c4.wait_send())
        c5 = ctx_copy(aguq.at[0], aguq.at[0], sa.at[i], ra.at[0], peer)
        maybe(own_cc == n, me < own_cc, lambda: c5.wait_send())

        @pl.when(me < kvl)
        def _():
            ctx_copy(agkv.at[0], agkv.at[0], s8.at[i], r8.at[0], peer).wait_send()

    for j in range(kvl):
        pl.when(me != j)(lambda: kv_send(j).wait_send())
    for i in range(1, nh):
        peer = lax.rem(mh + i, nh)
        head_copy(lowp, lowr.at[mh], s3.at[i], r3.at[mh], peer).wait_send()
        head_copy(backr.at[mh], backr.at[mh], s4.at[i], r4.at[mh], peer).wait_send()
    cp_dk.wait()
    cp_dv.wait()
    for j in range(kvl):
        cp_gq(j).wait()


def finish(*refs):
    src, dst, buf, wide = refs[:6], refs[6:12], refs[12:15], refs[15:18]
    in_sem, out_sem = refs[18:]
    loads, stores = [], []
    for a in range(3):
        stores.append(pltpu.make_async_copy(src[a], dst[a], out_sem.at[a]))
        loads.append(pltpu.make_async_copy(src[3 + a], buf[a], in_sem.at[a]))
    for c in stores + loads:
        c.start()
    for a, c in enumerate(loads):
        c.wait()
        wide[a][...] = buf[a][...].astype(F32)
        stores.append(pltpu.make_async_copy(wide[a], dst[3 + a], out_sem.at[3 + a]))
        stores[-1].start()
    for c in stores:
        c.wait()


def on_device(n, nh, hid, q, k, v, do, ad, uq, ukv):
    rows, cols = hid.shape
    kvl, R, own_st, cc, own_cc = dims_of(rows, cols, k.shape[1], n)
    nsub = rows // min(256, rows)
    total_tokens = rows * n
    hbm_spec = pl.BlockSpec(memory_space=pltpu.HBM)
    any_spec = pl.BlockSpec(memory_space=pl.ANY)
    vmem_spec = pl.BlockSpec(memory_space=pltpu.VMEM)
    V = pltpu.VMEM
    dma = pltpu.SemaphoreType.DMA
    kw = k.shape[1]
    r3 = 3 * RANK
    parts = pl.pallas_call(
        functools.partial(
            kernel, n, nh, 1.0 / math.sqrt(W * total_tokens), 1.0 / math.sqrt(total_tokens)
        ),
        out_shape=(
            jax.ShapeDtypeStruct((rows, cols), BF),
            jax.ShapeDtypeStruct((rows, kw), BF),
            jax.ShapeDtypeStruct((rows, kw), BF),
            jax.ShapeDtypeStruct((r3, cols), BF),
            jax.ShapeDtypeStruct((RANK, cols), BF),
            jax.ShapeDtypeStruct((2 * RANK, kw), BF),
        ),
        in_specs=[hbm_spec] * 8,
        out_specs=(any_spec, any_spec, any_spec, vmem_spec, vmem_spec, vmem_spec),
        scratch_shapes=[
            V((rows, cols), BF), V((rows, cols), BF), V((rows, kw), BF), V((rows, kw), BF),
            V((rows, cols), BF), V(ad.shape, BF), V(uq.shape, BF), V(ukv.shape, BF),
            V((rows, cols), BF), V((rows, kw), F32), V((rows, kw), F32),
            V((nsub, kvl * W, W), F32), V((nsub, kvl * W, W), F32),
            V((2, kvl * W, W), BF), V((n, 2, R, W), BF), V((n, 2, R, W), BF), V((2, kvl * W, W), BF),
            V((r3, rows), BF), V((nh, r3, rows), BF), V((r3, rows), BF),
            V((r3, rows), F32), V((nh, r3, rows), BF), V((r3, rows), BF),
            V((own_cc, r3, cc), BF), V((n, r3, cc), BF), V((own_cc, r3, cc), BF),
            V((own_cc, RANK, cc), BF), V((n, RANK, cc), BF), V((own_cc, RANK, cc), BF),
            V((kvl, 2 * RANK, W), BF), V((n, 2 * RANK, W), BF), V((kvl, 2 * RANK, W), BF),
            dma((6 + 2 * kvl,)), dma((2 + kvl,)),
            dma((n,)), dma((n,)), dma((n,)), dma((n,)),
            dma((nh,)), dma((nh,)), dma((nh,)), dma((nh,)),
            dma((n,)), dma((n,)), dma((n,)), dma((n,)),
            dma((kvl,)), dma((n,)), dma((n,)), dma((kvl,)),
            dma((own_cc,)), dma((n,)), dma((n,)), dma((own_cc,)),
        ],
        compiler_params=pltpu.CompilerParams(
            collective_id=0, has_side_effects=True, vmem_limit_bytes=34 * 1024 * 1024
        ),
        name="linear_attention_backward",
    )(*(pltpu.with_memory_space_constraint(x, pltpu.HBM) for x in (hid, q, k, v, do, ad, uq, ukv)))
    return pl.pallas_call(
        finish,
        out_shape=tuple(
            jax.ShapeDtypeStruct(p.shape, BF if at < 3 else F32) for at, p in enumerate(parts)
        ),
        in_specs=[any_spec] * 6,
        out_specs=(hbm_spec,) * 6,
        scratch_shapes=[V(p.shape, BF) for p in parts[3:]]
        + [V(p.shape, F32) for p in parts[3:]]
        + [dma((3,)), dma((6,))],
        compiler_params=pltpu.CompilerParams(vmem_limit_bytes=12 * 1024 * 1024),
        name="write_results",
    )(*parts)


def solution(mesh):
    tok, feat = P("ctx", "head"), P(None, "head")
    return jax.shard_map(
        functools.partial(on_device, mesh.shape["ctx"], mesh.shape["head"]),
        mesh=mesh,
        in_specs=(tok, tok, tok, tok, tok, feat, feat, feat),
        out_specs=(tok, tok, tok, feat, feat, feat),
        check_vma=False,
    )
```
